512 devices in a mesh: dp: 8 (over x, z_hi), tp: 16 (over z_lo, core), sec: 4 (over y).
Axes of the slice: x: 4, y: 4, z: 16 (z_hi: 2, z_lo: 8; z = z_hi * 8 + z_lo), core: 2. Of those that a mesh axis runs over, the one named last changes fastest.
Arguments:
- hidden_states: bfloat16 [4, 512, 8192], P(None, ('dp', 'sec')), may hold values from -6 to 6
- w_query: bfloat16 [8192, 8192], P(('dp', 'sec'), 'tp'), may hold values from -0.0625 to 0.0625
- w_keyval: bfloat16 [8192, 2048], P(('dp', 'sec'), 'tp'), may hold values from -0.0625 to 0.0625
- key_cache: bfloat16 [512, 16, 256, 128], P(('dp', 'sec'), 'tp'), may hold values from -200 to 200, as said below
- value_cache: bfloat16 [512, 16, 256, 128], P(('dp', 'sec'), 'tp'), may hold values from -6 to 6
- cache_begin: int32 [512], P(('dp', 'sec')), may hold values from 0 to 128
- cache_end: int32 [512], P(('dp', 'sec')), may hold values from 256 to 512
Outputs:
- handoff: bfloat16 [4, 512, 8192], P(None, 'dp', ('tp', 'sec'))
The draws below stay inside these ranges and needn't reach their ends.
Inputs may be any that keep to these rules, and one draw needn't show every extreme that they name: `key_cache`: cached keys; largest magnitudes differ between draws.
All inputs are finite; a program needn't handle non-finite values.
Results may differ from the reference program's by a relative error of at most 0.04.
Values may be sent and summed in bfloat16 or wider, within the bound.
No kernel may reach another device: no remote copies, remote signals or barrier semaphores. Data moves between devices by JAX's collectives and lax.ppermute only.
A program may use at most 64 MiB of HBM per device.

```python
import jax
import jax.numpy as jnp
from jax import lax

D = 8192
H = 64
KVH = 8
HD = 128
STEPS = 4
CACHE = 512
ROLLOUTS = 512


def draw_key_cache(key, part):
    base = jax.random.normal(key, (ROLLOUTS, 2 * KVH, CACHE // 2, HD), jnp.float32)
    return jnp.clip(base, -200.0, 200.0).astype(jnp.bfloat16)


def cache_bounds(key):
    begin = jax.random.randint(jax.random.fold_in(key, 11), (ROLLOUTS,), 0, CACHE // 4 + 1)
    finish = jax.random.randint(jax.random.fold_in(key, 12), (ROLLOUTS,), CACHE // 2, CACHE + 1)
    begin = begin.at[0].set(0).at[1].set(CACHE // 4)
    finish = finish.at[0].set(CACHE).at[1].set(CACHE // 2)
    return (begin.astype(jnp.int32), finish.astype(jnp.int32))


def draw_cache_begin(key, part):
    return cache_bounds(key)[0]


def draw_cache_end(key, part):
    return cache_bounds(key)[1]


def shard_levels(own_key, dims, shards, low, largest):
    def one(dim, blocks):
        steps = jax.random.uniform(jax.random.fold_in(jax.random.fold_in(own_key, 6), dim), (blocks,), jnp.float32, low / len(shards), largest / len(shards))
        return jnp.repeat(jnp.exp(steps), dims[dim] // blocks).reshape((-1,) + (1,) * (len(dims) - dim - 1))

    gain = one(*shards[0])
    for cut in shards[1:]:
        gain = gain * one(*cut)
    return gain


def noise(own_key, shape, deviation, most, cuts=(), held_as=jnp.bfloat16):
    drawn = jax.random.normal(own_key, shape, jnp.float32) * deviation
    if len(cuts) > 0:
        drawn = shard_levels(own_key, shape, cuts, -0.22, 0.18) * drawn
    return jnp.clip(drawn, min=-most, max=most).astype(held_as)


def setup_inputs(seed: int = 0) -> dict:
    key_list = jax.random.split(jax.random.key(seed), 8)
    return {
        "hidden_states": noise(key_list[0], (STEPS, ROLLOUTS, D), 1.0, 6.0, ((1, 32),)),
        "w_query": noise(key_list[1], (D, H * HD), D ** -0.5, 0.0625, ((0, 32), (1, 16))),
        "w_keyval": noise(key_list[2], (D, 2 * KVH * HD), D ** -0.5, 0.0625, ((0, 32), (1, 16))),
        "key_cache": draw_key_cache(jax.random.fold_in(key_list[7], 71), 0),
        "value_cache": noise(key_list[4], (ROLLOUTS, 2 * KVH, CACHE // 2, HD), 1.0, 6.0, ((0, 32), (1, 16))),
        "cache_begin": draw_cache_begin(jax.random.fold_in(key_list[7], 71), 0),
        "cache_end": draw_cache_end(jax.random.fold_in(key_list[7], 71), 0),
    }


THETA = 500000.0


def rotate(vector, positions):
    half = vector.shape[-1] // 2
    freq = THETA ** (-(jnp.arange(half, dtype=jnp.float32) * 2.0 / vector.shape[-1]))
    angle = positions[..., None] * freq
    angle = angle.reshape(positions.shape + (1,) * (vector.ndim - positions.ndim - 1) + (half,))
    cosine = jnp.cos(angle)
    sine = jnp.sin(angle)
    first = vector[..., :half]
    second = vector[..., half:]
    return jnp.concatenate([first * cosine - second * sine, second * cosine + first * sine], axis=-1)


def reference(hidden_states, w_query, w_keyval, key_cache, value_cache, cache_begin, cache_end):
    token_rows = hidden_states.reshape(STEPS * ROLLOUTS, D)
    positions = cache_end.astype(jnp.float32)[None, :] + jnp.arange(STEPS, dtype=jnp.float32)[:, None]
    query = jnp.dot(token_rows, w_query, preferred_element_type=jnp.float32).reshape(STEPS, ROLLOUTS, H, HD)
    query = rotate(query, positions).astype(jnp.bfloat16)
    keyval = jnp.dot(token_rows, w_keyval, preferred_element_type=jnp.float32).reshape(STEPS, ROLLOUTS, KVH, 2, HD)
    new_keys = rotate(keyval[:, :, :, 0], positions).astype(jnp.bfloat16)
    new_values = keyval[:, :, :, 1].astype(jnp.bfloat16)
    all_keys = key_cache.reshape(ROLLOUTS, KVH, CACHE, HD)
    all_values = value_cache.reshape(ROLLOUTS, KVH, CACHE, HD)
    group_size = H // KVH
    score_scale = HD ** -0.5
    cache_pos = jnp.arange(CACHE, dtype=jnp.int32)
    step_ids = jnp.arange(STEPS, dtype=jnp.int32)
    causal = step_ids[None, :] <= step_ids[:, None]

    def one_rollout(inputs):
        q_roll, k_roll, v_roll, nk_roll, nv_roll, begin, end = inputs
        q_float = q_roll.astype(jnp.float32).reshape(STEPS, KVH, group_size, HD)
        cache_scores = jnp.einsum('skgd,kpd->skgp', q_float, k_roll.astype(jnp.float32)) * score_scale
        new_scores = jnp.einsum('skgd,tkd->skgt', q_float, nk_roll.astype(jnp.float32)) * score_scale
        cache_live = (cache_pos >= begin) & (cache_pos < end)
        live = jnp.concatenate([
            jnp.broadcast_to(cache_live[None, None, None, :], cache_scores.shape),
            jnp.broadcast_to(causal[:, None, None, :], new_scores.shape)], axis=-1)
        scores = jnp.concatenate([cache_scores, new_scores], axis=-1)
        masked = jnp.where(live, scores, jnp.float32(-1e30))
        peak = jnp.max(masked, axis=-1, keepdims=True)
        expo = jnp.where(live, jnp.exp(masked - peak), jnp.float32(0.0))
        totals = jnp.sum(expo, axis=-1)
        probs = lax.optimization_barrier(expo.astype(jnp.bfloat16)).astype(jnp.float32)
        values = jnp.concatenate([v_roll.astype(jnp.float32), jnp.transpose(nv_roll.astype(jnp.float32), (1, 0, 2))], axis=1)
        weighted = jnp.einsum('skgp,kpd->skgd', probs, values) / totals[..., None]
        return weighted.astype(jnp.bfloat16).reshape(STEPS, H * HD)

    result = lax.map(one_rollout, (
        jnp.transpose(query, (1, 0, 2, 3)), all_keys, all_values,
        jnp.transpose(new_keys, (1, 0, 2, 3)), jnp.transpose(new_values, (1, 0, 2, 3)),
        cache_begin, cache_end))
    return jnp.transpose(result, (1, 0, 2))
```

```python
import jax
import jax.numpy as jnp
from jax import lax
from jax.experimental import pallas as pl
from jax.experimental.pallas import tpu as pltpu
from jax.sharding import Mesh, PartitionSpec as P

THETA = 500000.0
NEG = -1e30


def regroup(hidden, groups, pair, width):
    rows = hidden.shape[0]
    xs, secs = groups

    def kernel(h_ref, o_ref, sems):
        copies = []
        for x in range(xs):
            for s in range(secs):
                for h in range(pair):
                    src = ((x * pair + h) * secs + s) * width
                    copies.append(
                        pltpu.make_async_copy(
                            h_ref.at[:, pl.ds(src, width)],
                            o_ref.at[x * secs + s, :, pl.ds(h * width, width)],
                            sems.at[len(copies)],
                        )
                    )
        for c in copies:
            c.start()
        for c in copies:
            c.wait()

    return pl.pallas_call(
        kernel,
        out_shape=jax.ShapeDtypeStruct((xs * secs, rows, pair * width), hidden.dtype),
        in_specs=[pl.BlockSpec(memory_space=pl.ANY)],
        out_specs=pl.BlockSpec(memory_space=pltpu.VMEM),
        scratch_shapes=[pltpu.SemaphoreType.DMA((xs * secs * pair,))],
        cost_estimate=pl.CostEstimate(flops=0, bytes_accessed=2 * hidden.size * 2, transcendentals=0),
        name="regroup",
    )(hidden)


def project(tokens, w_own, k_own, w_other, k_other, half):
    groups, rows, feats = tokens.shape
    width = feats // 2
    q_cols = w_own.shape[1]
    kv_cols = k_own.shape[1]
    step = 4

    def kernel(half_ref, t_ref, wo_ref, ko_ref, wp_ref, kp_ref, o_ref):
        mine = pl.multiple_of(half_ref[0] * width, width)
        theirs = pl.multiple_of((1 - half_ref[0]) * width, width)
        a = t_ref[:, :, pl.ds(mine, width)].reshape(step * rows, width)
        b = t_ref[:, :, pl.ds(theirs, width)].reshape(step * rows, width)
        q = jnp.dot(a, wo_ref[...], preferred_element_type=jnp.float32)
        q = q + jnp.dot(b, wp_ref[...], preferred_element_type=jnp.float32)
        o_ref[:, :, pl.ds(0, q_cols)] = q.astype(jnp.bfloat16).reshape(step, rows, q_cols)
        k = jnp.dot(a, ko_ref[...], preferred_element_type=jnp.float32)
        k = k + jnp.dot(b, kp_ref[...], preferred_element_type=jnp.float32)
        o_ref[:, :, pl.ds(q_cols, kv_cols)] = k.astype(jnp.bfloat16).reshape(step, rows, kv_cols)

    def whole(a):
        return pl.BlockSpec(a.shape, lambda i, h: (0, 0))

    return pl.pallas_call(
        kernel,
        out_shape=jax.ShapeDtypeStruct((groups, rows, q_cols + kv_cols), jnp.bfloat16),
        grid_spec=pltpu.PrefetchScalarGridSpec(
            num_scalar_prefetch=1,
            grid=(groups // step,),
            in_specs=[
                pl.BlockSpec((step, rows, feats), lambda i, h: (i, 0, 0)),
                whole(w_own),
                whole(k_own),
                whole(w_other),
                whole(k_other),
            ],
            out_specs=pl.BlockSpec((step, rows, q_cols + kv_cols), lambda i, h: (i, 0, 0)),
        ),
        name="project",
    )(half, tokens, w_own, k_own, w_other, k_other)


def finish_projection(parts, cosine, sine, parity, heads, steps):
    groups, rows, cols = parts.shape
    size = cosine.shape[1]
    batch = rows // steps

    def kernel(par_ref, p_ref, c_ref, s_ref, q_ref, kv_ref, qf, kvf):
        total = p_ref[0].astype(jnp.float32)
        for g in range(1, groups):
            total = total + p_ref[g].astype(jnp.float32)
        cos = c_ref[...]
        sin = s_ref[...]

        def rope(v):
            return v * cos + pltpu.roll(v, size // 2, 1) * sin

        own = total[:, heads * size :]
        own = jnp.where(par_ref[0] == 0, rope(own), own)
        kvf[...] = own.astype(jnp.bfloat16).astype(jnp.float32)
        for h in range(heads):
            qf[h] = rope(total[:, h * size : (h + 1) * size])
        for b in range(batch):
            kv_ref[b] = kvf[pl.ds(b, steps, stride=batch), :]
            per_head = [qf[h, pl.ds(b, steps, stride=batch), :] for h in range(heads)]
            q_ref[b] = jnp.concatenate(per_head, axis=0).astype(jnp.bfloat16)

    vm = pl.BlockSpec(memory_space=pltpu.VMEM)
    return pl.pallas_call(
        kernel,
        out_shape=(
            jax.ShapeDtypeStruct((batch, heads * steps, size), jnp.bfloat16),
            jax.ShapeDtypeStruct((batch, steps, size), jnp.float32),
        ),
        in_specs=[pl.BlockSpec(memory_space=pltpu.SMEM), vm, vm, vm],
        out_specs=(vm, vm),
        scratch_shapes=[
            pltpu.VMEM((heads, rows, size), jnp.float32),
            pltpu.VMEM((rows, size), jnp.float32),
        ],
        name="finish_projection",
    )(parity, parts, cosine, sine)


def attend(scalars, query, own_kv, other_kv, k_own, k_other, v_own, v_other, steps):
    batch, q_rows, size = query.shape
    heads = q_rows // steps
    half_len = k_own.shape[2]
    scale = size ** (-0.5)
    block = 4
    rows = steps * batch
    nt = (((1,), (1,)), ((), ()))

    def kernel(s_ref, q_ref, mine_ref, theirs_ref, ka_ref, kb_ref, va_ref, vb_ref, o_ref, acc):
        i = pl.program_id(0)
        parity = s_ref[0]
        key_first = parity == 0
        pos = lax.broadcasted_iota(jnp.int32, (q_rows, half_len), 1)
        pos_a = pos + parity * half_len
        pos_b = pos + (1 - parity) * half_len
        step_row = lax.broadcasted_iota(jnp.int32, (q_rows, steps), 0) % steps
        causal = lax.broadcasted_iota(jnp.int32, (q_rows, steps), 1) <= step_row
        for j in range(block):
            b = i * block + j
            begin = s_ref[1 + b]
            end = s_ref[1 + batch + b]
            q = q_ref[j]
            mine = mine_ref[j]
            theirs = theirs_ref[j]
            new_k = jnp.where(key_first, mine, theirs).astype(jnp.bfloat16)
            new_v = jnp.where(key_first, theirs, mine).astype(jnp.bfloat16)
            live_a = (pos_a >= begin) & (pos_a < end)
            live_b = (pos_b >= begin) & (pos_b < end)
            sa = lax.dot_general(q, ka_ref[j, 0], nt, preferred_element_type=jnp.float32) * scale
            sb = lax.dot_general(q, kb_ref[j, 0], nt, preferred_element_type=jnp.float32) * scale
            sn = lax.dot_general(q, new_k, nt, preferred_element_type=jnp.float32) * scale
            sa = jnp.where(live_a, sa, NEG)
            sb = jnp.where(live_b, sb, NEG)
            sn = jnp.where(causal, sn, NEG)
            peak = jnp.maximum(
                jnp.max(jnp.maximum(sa, sb), axis=-1, keepdims=True),
                jnp.max(sn, axis=-1, keepdims=True),
            )
            ea = jnp.where(live_a, jnp.exp(sa - peak), 0.0)
            eb = jnp.where(live_b, jnp.exp(sb - peak), 0.0)
            en = jnp.where(causal, jnp.exp(sn - peak), 0.0)
            total = jnp.sum(ea + eb, axis=-1, keepdims=True) + jnp.sum(en, axis=-1, keepdims=True)
            w = jnp.dot(ea.astype(jnp.bfloat16), va_ref[j, 0], preferred_element_type=jnp.float32)
            w = w + jnp.dot(eb.astype(jnp.bfloat16), vb_ref[j, 0], preferred_element_type=jnp.float32)
            w = w + jnp.dot(en.astype(jnp.bfloat16), new_v, preferred_element_type=jnp.float32)
            w = w / total
            for h in range(heads):
                acc[pl.ds(h * rows + b, steps, stride=batch), :] = w[h * steps : (h + 1) * steps]

        @pl.when(i == pl.num_programs(0) - 1)
        def _():
            o_ref[...] = acc[...].astype(jnp.bfloat16).reshape(heads, rows, size)

    def per(a):
        return pl.BlockSpec((block,) + a.shape[1:], lambda i, s: (i,) + (0,) * (a.ndim - 1))

    return pl.pallas_call(
        kernel,
        out_shape=jax.ShapeDtypeStruct((heads, rows, size), jnp.bfloat16),
        grid_spec=pltpu.PrefetchScalarGridSpec(
            num_scalar_prefetch=1,
            grid=(batch // block,),
            in_specs=[per(a) for a in (query, own_kv, other_kv, k_own, k_other, v_own, v_other)],
            out_specs=pl.BlockSpec((heads, rows, size), lambda i, s: (0, 0, 0)),
            scratch_shapes=[pltpu.VMEM((heads * rows, size), jnp.float32)],
        ),
        name="attend",
    )(scalars, query, own_kv, other_kv, k_own, k_other, v_own, v_other)


def body(hidden_states, w_query, w_keyval, key_cache, value_cache, cache_begin, cache_end):
    steps, batch, width = hidden_states.shape
    size = key_cache.shape[-1]
    heads = w_query.shape[1] // size
    xs, zs, secs = lax.axis_size("x"), lax.axis_size("zh"), lax.axis_size("sec")
    half = lax.axis_index("zh").astype(jnp.int32)
    parity = lax.axis_index("core").astype(jnp.int32)
    swap = [(0, 1), (1, 0)]

    w_other = lax.ppermute(w_query, "zh", swap)
    k_other = lax.ppermute(w_keyval, "zh", swap)
    keys_other = lax.ppermute(key_cache, "core", swap)
    values_other = lax.ppermute(value_cache, "core", swap)

    grouped = regroup(
        hidden_states.reshape(steps * batch, width), (xs, secs), zs, w_query.shape[0]
    )
    tokens = lax.all_to_all(grouped, ("x", "sec"), 0, 0, tiled=True)
    partial = project(tokens, w_query, w_keyval, w_other, k_other, half.reshape(1))
    parts = lax.all_to_all(partial, ("x", "sec"), 0, 0, tiled=True)

    position = (
        cache_end.astype(jnp.float32)[None, :] + jnp.arange(steps, dtype=jnp.float32)[:, None]
    ).reshape(steps * batch, 1)
    freq = THETA ** (-(jnp.arange(size // 2, dtype=jnp.float32) * 2.0 / size))
    angle = position * freq
    cosine = jnp.cos(angle)
    sine = jnp.sin(angle)
    cosine = jnp.concatenate([cosine, cosine], axis=1)
    sine = jnp.concatenate([-sine, sine], axis=1)

    query, own_kv = finish_projection(parts, cosine, sine, parity.reshape(1), heads, steps)
    other_kv = lax.ppermute(own_kv, "core", swap)
    scalars = jnp.concatenate([parity.reshape(1), cache_begin, cache_end])
    attended = attend(
        scalars, query, own_kv, other_kv, key_cache, keys_other, value_cache, values_other, steps
    )
    handed = lax.all_to_all(attended, "sec", 0, 0, tiled=True)
    handed = handed.reshape(secs, steps, batch, size)
    return jnp.transpose(handed, (1, 0, 2, 3)).reshape(steps, secs * batch, size)


def solution(mesh):
    dp, tp, sec = (mesh.shape[a] for a in ("dp", "tp", "sec"))
    fine = Mesh(mesh.devices.reshape(dp // 2, 2, tp // 2, 2, sec), ("x", "zh", "zl", "core", "sec"))
    rows, cols = ("x", "zh", "sec"), ("zl", "core")
    return jax.shard_map(
        body,
        mesh=fine,
        in_specs=(
            P(None, rows, None),
            P(rows, cols),
            P(rows, cols),
            P(rows, cols, None, None),
            P(rows, cols, None, None),
            P(rows),
            P(rows),
        ),
        out_specs=P(None, ("x", "zh"), ("zl", "core", "sec")),
        check_vma=False,
    )
```

```python
import jax
import jax.numpy as jnp
from jax import lax
from jax.experimental import pallas as pl
from jax.experimental.pallas import tpu as pltpu
from jax.sharding import Mesh, PartitionSpec as P

THETA = 500000.0
NEG = -1e30


def limits(mib):
    return pltpu.CompilerParams(vmem_limit_bytes=mib << 20)


def regroup(hidden, w_query, w_keyval, groups, pair):
    rows = hidden.shape[0]
    xs, secs = groups
    width, q_cols = w_query.shape
    kv_cols = w_keyval.shape[1]

    def kernel(h_ref, q_ref, k_ref, o_ref, w_ref, sems):
        copies = []

        def add(src, dst):
            copies.append(pltpu.make_async_copy(src, dst, sems.at[len(copies)]))

        for x in range(xs):
            for s in range(secs):
                for h in range(pair):
                    at = ((x * pair + h) * secs + s) * width
                    add(
                        h_ref.at[:, pl.ds(at, width)],
                        o_ref.at[x * secs + s, :, pl.ds(h * width, width)],
                    )
        add(q_ref, w_ref.at[:, pl.ds(0, q_cols)])
        add(k_ref, w_ref.at[:, pl.ds(q_cols, kv_cols)])
        for c in copies:
            c.start()
        for c in copies:
            c.wait()

    hbm = pl.BlockSpec(memory_space=pl.ANY)
    vm = pl.BlockSpec(memory_space=pltpu.VMEM)
    return pl.pallas_call(
        kernel,
        out_shape=(
            jax.ShapeDtypeStruct((xs * secs, rows, pair * width), hidden.dtype),
            jax.ShapeDtypeStruct((width, q_cols + kv_cols), w_query.dtype),
        ),
        in_specs=[hbm, hbm, hbm],
        out_specs=(vm, vm),
        scratch_shapes=[pltpu.SemaphoreType.DMA((xs * secs * pair + 2,))],
        name="regroup",
    )(hidden, w_query, w_keyval)


def project(half, tokens, w_own, w_other):
    groups, rows, feats = tokens.shape
    width, cols = w_own.shape
    step = 4

    def kernel(half_ref, t_ref, wo_ref, wp_ref, o_ref):
        mine = pl.multiple_of(half_ref[0] * width, width)
        theirs = pl.multiple_of((1 - half_ref[0]) * width, width)
        for g in range(0, groups, step):
            a = t_ref[g : g + step, :, pl.ds(mine, width)].reshape(step * rows, width)
            b = t_ref[g : g + step, :, pl.ds(theirs, width)].reshape(step * rows, width)
            y = jnp.dot(a, wo_ref[...], preferred_element_type=jnp.float32)
            y = y + jnp.dot(b, wp_ref[...], preferred_element_type=jnp.float32)
            o_ref[g : g + step] = y.astype(jnp.bfloat16).reshape(step, rows, cols)

    vm = pl.BlockSpec(memory_space=pltpu.VMEM)
    return pl.pallas_call(
        kernel,
        out_shape=jax.ShapeDtypeStruct((groups, rows, cols), jnp.bfloat16),
        in_specs=[pl.BlockSpec(memory_space=pltpu.SMEM), vm, vm, vm],
        out_specs=vm,
        compiler_params=limits(16),
        name="project",
    )(half, tokens, w_own, w_other)


def reorder(n, batch, heads, steps, to_batch):
    a = lax.broadcasted_iota(jnp.int32, (n, n), 0 if to_batch else 1)
    c = lax.broadcasted_iota(jnp.int32, (n, n), 1 if to_batch else 0)
    from_a = (a % (heads * steps)) * batch + a // (heads * steps)
    return (from_a == c).astype(jnp.float32).astype(jnp.bfloat16)


def finish_projection(parity, parts, cosine, sine, heads, steps):
    groups, rows, _ = parts.shape
    size = cosine.shape[1]
    batch = rows // steps

    def kernel(par_ref, p_ref, c_ref, s_ref, q_ref, kv_ref):
        cos = c_ref[...]
        sin = s_ref[...]

        def rope(v):
            return v * cos + pltpu.roll(v, size // 2, 1) * sin

        def summed(h):
            total = p_ref[0, :, h * size : (h + 1) * size].astype(jnp.float32)
            for g in range(1, groups):
                total = total + p_ref[g, :, h * size : (h + 1) * size].astype(jnp.float32)
            return total

        own = summed(heads)
        kv_ref[...] = jnp.where(par_ref[0] == 0, rope(own), own).astype(jnp.bfloat16)
        q = jnp.concatenate([rope(summed(h)).astype(jnp.bfloat16) for h in range(heads)], axis=0)
        order = reorder(heads * rows, batch, heads, steps, True)
        q_ref[...] = jnp.dot(order, q, preferred_element_type=jnp.float32).astype(jnp.bfloat16)

    vm = pl.BlockSpec(memory_space=pltpu.VMEM)
    return pl.pallas_call(
        kernel,
        out_shape=(
            jax.ShapeDtypeStruct((heads * rows, size), jnp.bfloat16),
            jax.ShapeDtypeStruct((rows, size), jnp.bfloat16),
        ),
        in_specs=[pl.BlockSpec(memory_space=pltpu.SMEM), vm, vm, vm],
        out_specs=(vm, vm),
        compiler_params=limits(16),
        name="finish_projection",
    )(parity, parts, cosine, sine)


def attend(parity, begin, end, query, own_kv, other_kv, k_own, k_other, v_own, v_other, steps):
    n, size = query.shape
    rows = own_kv.shape[0]
    batch = rows // steps
    per = n // batch
    heads = per // steps
    half_len = k_own.shape[2]
    scale = size ** (-0.5)
    block = 4
    nt = (((1,), (1,)), ((), ()))

    def kernel(
        par_ref, begin_ref, end_ref, q_ref, mine_ref, theirs_ref, ka, kb, va, vb, o_ref
    ):
        key_first = par_ref[0] == 0
        offset_a = par_ref[0] * half_len
        offset_b = half_len - offset_a
        new_k = jnp.where(key_first, mine_ref[...], theirs_ref[...])
        new_v = jnp.where(key_first, theirs_ref[...], mine_ref[...])
        pos = lax.broadcasted_iota(jnp.int32, (per, half_len), 1)
        done = []
        for i in range(0, batch, block):
            lo, m = i * per, block * per
            q = q_ref[lo : lo + m]
            sa, sb = [], []
            for b in range(i, i + block):
                qb = q_ref[b * per : (b + 1) * per]
                for keys, offset, out in ((ka, offset_a, sa), (kb, offset_b, sb)):
                    s = lax.dot_general(qb, keys[b, 0], nt, preferred_element_type=jnp.float32)
                    live = (pos >= begin_ref[b] - offset) & (pos < end_ref[b] - offset)
                    out.append(jnp.where(live, s * scale, NEG))
            sa = jnp.concatenate(sa, axis=0)
            sb = jnp.concatenate(sb, axis=0)
            sn = lax.dot_general(q, new_k, nt, preferred_element_type=jnp.float32) * scale
            r = lax.broadcasted_iota(jnp.int32, (m, rows), 0) + lo
            c = lax.broadcasted_iota(jnp.int32, (m, rows), 1)
            seen = (c % batch == r // per) & (c // batch <= r % steps)
            sn = jnp.where(seen, sn, NEG)
            peak = jnp.maximum(
                jnp.max(jnp.maximum(sa, sb), axis=-1, keepdims=True),
                jnp.max(sn, axis=-1, keepdims=True),
            )
            ea = jnp.exp(sa - peak)
            eb = jnp.exp(sb - peak)
            en = jnp.exp(sn - peak)
            total = jnp.sum(ea + eb, axis=-1, keepdims=True) + jnp.sum(en, axis=-1, keepdims=True)
            ea = ea.astype(jnp.bfloat16)
            eb = eb.astype(jnp.bfloat16)
            w = []
            for j in range(block):
                part = slice(j * per, (j + 1) * per)
                wa = jnp.dot(ea[part], va[i + j, 0], preferred_element_type=jnp.float32)
                wb = jnp.dot(eb[part], vb[i + j, 0], preferred_element_type=jnp.float32)
                w.append(wa + wb)
            w = jnp.concatenate(w, axis=0)
            w = w + jnp.dot(en.astype(jnp.bfloat16), new_v, preferred_element_type=jnp.float32)
            done.append((w / total).astype(jnp.bfloat16))
        order = reorder(n, batch, heads, steps, False)
        out = jnp.dot(order, jnp.concatenate(done, axis=0), preferred_element_type=jnp.float32)
        o_ref[...] = out.astype(jnp.bfloat16).reshape(heads, rows, size)

    vm = pl.BlockSpec(memory_space=pltpu.VMEM)
    sm = pl.BlockSpec(memory_space=pltpu.SMEM)
    return pl.pallas_call(
        kernel,
        out_shape=jax.ShapeDtypeStruct((heads, rows, size), jnp.bfloat16),
        in_specs=[sm] * 3 + [vm] * 7,
        out_specs=vm,
        compiler_params=limits(24),
        name="attend",
    )(parity, begin, end, query, own_kv, other_kv, k_own, k_other, v_own, v_other)


def body(hidden_states, w_query, w_keyval, key_cache, value_cache, cache_begin, cache_end):
    steps, batch, width = hidden_states.shape
    size = key_cache.shape[-1]
    heads = w_query.shape[1] // size
    xs, zs, secs = lax.axis_size("x"), lax.axis_size("zh"), lax.axis_size("sec")
    half = lax.axis_index("zh").astype(jnp.int32).reshape(1)
    parity = lax.axis_index("core").astype(jnp.int32).reshape(1)
    swap = [(0, 1), (1, 0)]

    grouped, w_own = regroup(
        hidden_states.reshape(steps * batch, width), w_query, w_keyval, (xs, secs), zs
    )
    keys_other = lax.ppermute(key_cache, "core", swap)
    values_other = lax.ppermute(value_cache, "core", swap)
    tokens = lax.all_to_all(grouped, ("x", "sec"), 0, 0, tiled=True)
    w_other = lax.ppermute(w_own, "zh", swap)
    partial = project(half, tokens, w_own, w_other)
    parts = lax.all_to_all(partial, ("x", "sec"), 0, 0, tiled=True)

    position = (
        cache_end.astype(jnp.float32)[None, :] + jnp.arange(steps, dtype=jnp.float32)[:, None]
    ).reshape(steps * batch, 1)
    freq = THETA ** (-(jnp.arange(size // 2, dtype=jnp.float32) * 2.0 / size))
    angle = position * freq
    cosine = jnp.cos(angle)
    sine = jnp.sin(angle)
    cosine = jnp.concatenate([cosine, cosine], axis=1)
    sine = jnp.concatenate([-sine, sine], axis=1)

    query, own_kv = finish_projection(parity, parts, cosine, sine, heads, steps)
    other_kv = lax.ppermute(own_kv, "core", swap)
    attended = attend(
        parity,
        cache_begin,
        cache_end,
        query,
        own_kv,
        other_kv,
        key_cache,
        keys_other,
        value_cache,
        values_other,
        steps,
    )
    handed = lax.all_to_all(attended, "sec", 0, 0, tiled=True)
    handed = handed.reshape(secs, steps, batch, size)
    return jnp.transpose(handed, (1, 0, 2, 3)).reshape(steps, secs * batch, size)


def solution(mesh):
    dp, tp, sec = (mesh.shape[a] for a in ("dp", "tp", "sec"))
    fine = Mesh(mesh.devices.reshape(dp // 2, 2, tp // 2, 2, sec), ("x", "zh", "zl", "core", "sec"))
    rows, cols = ("x", "zh", "sec"), ("zl", "core")
    return jax.shard_map(
        body,
        mesh=fine,
        in_specs=(
            P(None, rows, None),
            P(rows, cols),
            P(rows, cols),
            P(rows, cols, None, None),
            P(rows, cols, None, None),
            P(rows),
            P(rows),
        ),
        out_specs=P(None, ("x", "zh"), ("zl", "core", "sec")),
        check_vma=False,
    )
```
